32 devices in a mesh: seq: 8 (over z, y), head: 4 (over x, core).
Axes of the slice: x: 2, y: 2, z: 4, core: 2. Of those that a mesh axis runs over, the one named last changes fastest.
Arguments:
- block_in: bfloat16 [1, 2048, 1024], P(None, 'seq'), may hold values from -6 to 6
- upstream: bfloat16 [1, 2048, 1024], P(None, 'seq'), may hold values from -6 to 6
- first_gain: float32 [1024], replicated, may hold values from 0.5 to 1.5
- project_in: bfloat16 [1024, 4, 512], P(None, 'head'), may hold values from -0.1875 to 0.1875
- filter_taps: float32 [4, 4, 512], P(None, 'head'), may hold values from -2 to 2
- squeeze: bfloat16 [1024, 16], replicated, may hold values from -0.1875 to 0.1875
- expand: bfloat16 [16, 512], P(None, 'head'), may hold values from -0.75 to 0.75
- decay_bias: float32 [512], P('head'), may hold values from 0 to 16
- gating: bfloat16 [1024, 1024], P(None, 'head'), may hold values from -0.1875 to 0.1875
- head_scale: float32 [256], replicated, may hold values from 0.5 to 1.5
- project_out: bfloat16 [1024, 1024], P('head'), may hold values from -0.375 to 0.375
- second_gain: float32 [1024], replicated, may hold values from 0.5 to 1.5
- hidden_gate: bfloat16 [1024, 2816], P(None, 'head'), may hold values from -0.1875 to 0.1875
- hidden_lift: bfloat16 [1024, 2816], P(None, 'head'), may hold values from -0.1875 to 0.1875
- hidden_drop: bfloat16 [2816, 1024], P('head'), may hold values from -0.15625 to 0.15625
Outputs:
- block_out: bfloat16 [1, 2048, 1024], P(None, 'seq')
- input_grad: float32 [1, 2048, 1024], P(None, 'seq')
- grad_first: float32 [1024], replicated
- grad_project: float32 [1024, 4, 512], P('seq', 'head')
- grad_taps: float32 [4, 4, 512], P(None, 'head')
- grad_squeeze: float32 [1024, 16], replicated
- grad_expand: float32 [16, 512], P(None, 'head')
- grad_bias: float32 [512], P('head')
- grad_gating: float32 [1024, 1024], P('seq', 'head')
- grad_scale: float32 [256], replicated
- grad_output: float32 [1024, 1024], P('head', 'seq')
- grad_second: float32 [1024], replicated
- grad_gate: float32 [1024, 2816], P('seq', 'head')
- grad_lift: float32 [1024, 2816], P('seq', 'head')
- grad_drop: float32 [2816, 1024], P('head', 'seq')
The draws below stay inside these ranges and needn't reach their ends.
All inputs are finite; a program needn't handle non-finite values.
Results may differ from the reference program's by a relative error of at most 0.02.
Values sent between devices are 32-bit elements; how exact they have to be, the bound alone decides.
A program may use at most 128 MiB of HBM per device.

```python
import math
import jax
import jax.numpy as jnp
from jax import lax

D = 1024
H = 4
DK = 128
DV = 256
FF = 2816
RANK = 16
CONV = 4
GROUP = 64
SEQS = 1
QKV = 512
LENGTH = 2048


def draw_decay_bias(key, part):
    first, second, third = jax.random.split(key, 3)
    pick = jax.random.uniform(first, (H * DK,), jnp.float32)
    share = 0.5
    slow = jnp.exp(jax.random.uniform(second, (H * DK,), jnp.float32, math.log(0.2 / LENGTH), math.log(1.2 / LENGTH)))
    quick = jnp.exp(jax.random.uniform(third, (H * DK,), jnp.float32, math.log(1.0 / 200.0), math.log(1.0 / 25.0)))
    rate = jnp.where(pick < share, slow, quick)
    return -jnp.log(jnp.expm1(16.0 * rate))


def block_scale(rng, extent, pieces, smallest, high):
    def one(axis_at, parts):
        heights = jax.random.uniform(jax.random.fold_in(jax.random.fold_in(rng, 6), axis_at), (parts,), jnp.float32, smallest / len(pieces), high / len(pieces))
        return jnp.repeat(jnp.exp(heights), extent[axis_at] // parts).reshape((-1,) + (1,) * (len(extent) - axis_at - 1))

    level = one(*pieces[0])
    for cut in pieces[1:]:
        level = level * one(*cut)
    return level


def normal_values(rng, dims, width, reach, shards=(), held_as=jnp.bfloat16):
    result = width * jax.random.normal(rng, dims, jnp.float32)
    if shards:
        result = result * block_scale(rng, dims, shards, -0.22, 0.18)
    return jnp.clip(result, -reach, reach).astype(held_as)


def setup_inputs(seed: int = 0) -> dict:
    splits = jax.random.split(jax.random.key(seed), 16)
    return {
        "block_in": normal_values(splits[0], (SEQS, LENGTH, D), 1.0, 6.0, ((1, 8),)),
        "upstream": normal_values(splits[1], (SEQS, LENGTH, D), 1.0, 6.0, ((1, 8),)),
        "first_gain": jnp.clip(1.0 + 0.1 * jax.random.normal(splits[2], (D,), jnp.float32), 0.5, 1.5),
        "project_in": normal_values(splits[3], (D, H, QKV), D ** -0.5, 0.1875, ((1, 4),)),
        "filter_taps": normal_values(splits[4], (CONV, H, QKV), 0.5, 2.0, ((1, 4),), jnp.float32),
        "squeeze": normal_values(splits[5], (D, RANK), D ** -0.5, 0.1875),
        "expand": normal_values(splits[6], (RANK, H * DK), (4 * RANK) ** -0.5, 0.75, ((1, 4),)),
        "decay_bias": draw_decay_bias(jax.random.fold_in(splits[15], 71), 0),
        "gating": normal_values(splits[8], (D, H * DV), D ** -0.5, 0.1875, ((1, 4),)),
        "head_scale": jnp.clip(1.0 + 0.1 * jax.random.normal(splits[9], (DV,), jnp.float32), 0.5, 1.5),
        "project_out": normal_values(splits[10], (H * DV, D), DV ** -0.5, 0.375, ((0, 4),)),
        "second_gain": jnp.clip(1.0 + 0.1 * jax.random.normal(splits[11], (D,), jnp.float32), 0.5, 1.5),
        "hidden_gate": normal_values(splits[12], (D, FF), D ** -0.5, 0.1875, ((1, 4),)),
        "hidden_lift": normal_values(splits[13], (D, FF), D ** -0.5, 0.1875, ((1, 4),)),
        "hidden_drop": normal_values(splits[14], (FF, D), (FF // 2) ** -0.5, 0.15625, ((0, 4),)),
    }


EPS = 1e-05
NORMALIZER = 16.0
HIGH = lax.Precision.HIGHEST

def product(left, right):
    return jnp.dot(left, right, preferred_element_type=jnp.float32)

def rms_scale(values):
    return lax.rsqrt(lax.optimization_barrier(jnp.mean(values * values, axis=-1, keepdims=True)) + EPS)

def rms_back(values, scale, gain, incoming):
    weighted = gain * incoming
    cube = scale * scale * scale
    return scale * weighted - values * cube * lax.optimization_barrier(jnp.mean(values * weighted, axis=-1, keepdims=True))

def silu_grad(values):
    logistic = jax.nn.sigmoid(values)
    return logistic * (1.0 + values * (1.0 - logistic))

def causal_mask():
    rows = lax.broadcasted_iota(jnp.int32, (GROUP, GROUP), 0)
    columns = lax.broadcasted_iota(jnp.int32, (GROUP, GROUP), 1)
    return (columns <= rows).astype(jnp.float32)

def group_view(array):
    return array.reshape((array.shape[0] // GROUP, GROUP) + array.shape[1:])

def run_states(decays, updates, backward):

    def step(carry, item):
        decay, update = item
        return (jnp.exp(decay)[..., None] * carry + update, carry)
    init = jnp.zeros(updates.shape[1:], jnp.float32)
    _, states = lax.scan(step, init, (decays, updates), reverse=backward)
    return states

def attention_parts(query, keys, log_decay):
    running = jnp.cumsum(group_view(log_decay), axis=1)
    last = running[:, -1]
    query_in = group_view(query) * jnp.exp(running)
    key_in = group_view(keys) * jnp.exp(-running)
    key_end = group_view(keys) * jnp.exp(last[:, None] - running)
    return (running, last, query_in, key_in, key_end)

def linear_attention(query, keys, values, log_decay):
    running, last, query_in, key_in, key_end = attention_parts(query, keys, log_decay)
    group_values = group_view(values)
    scores = jnp.einsum('nihc,njhc->nhij', query_in, key_in, precision=HIGH) * causal_mask()
    updates = jnp.einsum('njhc,njhd->nhcd', key_end, group_values, precision=HIGH)
    starts = run_states(last, updates, False)
    mixed = jnp.einsum('nhij,njhd->nihd', scores, group_values, precision=HIGH)
    mixed = mixed + jnp.einsum('nihc,nhcd->nihd', query_in, starts, precision=HIGH)
    return (mixed.reshape(values.shape), starts)

def attention_back(query, keys, values, log_decay, starts, grad_mixed):
    running, last, query_in, key_in, key_end = attention_parts(query, keys, log_decay)
    group_values = group_view(values)
    outgrad = group_view(grad_mixed)
    mask = causal_mask()
    scores = jnp.einsum('nihc,njhc->nhij', query_in, key_in, precision=HIGH) * mask
    query_end = jnp.einsum('nihc,nihd->nhcd', query_in, outgrad, precision=HIGH)
    following = run_states(last, query_end, True)
    inner_group = jnp.einsum('nihd,njhd->nhij', outgrad, group_values, precision=HIGH) * mask
    grad_query = jnp.exp(running) * (jnp.einsum('nhij,njhc->nihc', inner_group, key_in, precision=HIGH) + jnp.einsum('nihd,nhcd->nihc', outgrad, starts, precision=HIGH))
    grad_keys = jnp.exp(-running) * jnp.einsum('nhij,nihc->njhc', inner_group, query_in, precision=HIGH)
    grad_keys = grad_keys + jnp.exp(last[:, None] - running) * jnp.einsum('njhd,nhcd->njhc', group_values, following, precision=HIGH)
    grad_values = jnp.einsum('nhij,nihd->njhd', scores, outgrad, precision=HIGH)
    grad_values = grad_values + jnp.einsum('njhc,nhcd->njhd', key_end, following, precision=HIGH)
    grad_running = group_view(query) * grad_query - group_view(keys) * grad_keys
    flat = grad_running.reshape(log_decay.shape)
    grad_log = jnp.flip(jnp.cumsum(jnp.flip(flat, 0), axis=0), 0)
    return (grad_query.reshape(query.shape), grad_keys.reshape(keys.shape), grad_values.reshape(values.shape), grad_log)

def causal_conv(projected, taps):
    length = projected.shape[0]
    lags = taps.shape[0] - 1
    padded = jnp.concatenate([jnp.zeros((lags,) + projected.shape[1:], jnp.float32), projected], axis=0)
    total = jnp.zeros_like(projected)
    for lag in range(lags + 1):
        total = total + taps[lag] * padded[lags - lag:lags - lag + length]
    return (total, padded)

def conv_back(padded, taps, grad_filtered):
    length = grad_filtered.shape[0]
    lags = taps.shape[0] - 1
    padded_back = jnp.concatenate([grad_filtered, jnp.zeros((lags,) + grad_filtered.shape[1:], jnp.float32)], axis=0)
    grad_projected = jnp.zeros_like(grad_filtered)
    tap_rows = []
    for lag in range(lags + 1):
        grad_projected = grad_projected + taps[lag] * padded_back[lag:lag + length]
        tap_rows.append(lax.optimization_barrier(jnp.sum(grad_filtered * padded[lags - lag:lags - lag + length], axis=0)))
    return (grad_projected, jnp.stack(tap_rows))

def one_sequence(block_in, upstream, first_gain, project_in, filter_taps, squeeze, expand, decay_bias, gating, head_scale, project_out, second_gain, hidden_gate, hidden_lift, hidden_drop):
    length = block_in.shape[0]
    residual_in = block_in.astype(jnp.float32)
    scale_one = rms_scale(residual_in)
    normed_one = (residual_in * scale_one * first_gain).astype(jnp.bfloat16)
    weight_in = project_in.reshape(D, H * QKV)
    projected = product(normed_one, weight_in).reshape(length, H, QKV)
    filtered, padded = causal_conv(projected, filter_taps)
    activated_low = jax.nn.silu(filtered).astype(jnp.bfloat16)
    activated = lax.optimization_barrier(activated_low).astype(jnp.float32)
    root = DK ** (-0.5)
    query = activated[..., :DK] * root
    keys = activated[..., DK:2 * DK]
    values = activated[..., 2 * DK:]
    squeezed = product(normed_one, squeeze).astype(jnp.bfloat16)
    logits = product(squeezed, expand) + decay_bias
    log_decay = (jax.nn.log_sigmoid(logits) / NORMALIZER).reshape(length, H, DK)
    gate_in = product(normed_one, gating).reshape(length, H, DV)
    mixed, starts = linear_attention(query, keys, values, log_decay)
    scale_head = rms_scale(mixed)
    normed_head = mixed * scale_head * head_scale
    gated = (normed_head * jax.nn.silu(gate_in)).astype(jnp.bfloat16).reshape(length, H * DV)
    residual = residual_in + product(gated, project_out)
    scale_two = rms_scale(residual)
    normed_two = (residual * scale_two * second_gain).astype(jnp.bfloat16)
    gate_value = product(normed_two, hidden_gate)
    lift_value = product(normed_two, hidden_lift)
    inner = (jax.nn.silu(gate_value) * lift_value).astype(jnp.bfloat16)
    block_out = (residual + product(inner, hidden_drop)).astype(jnp.bfloat16)
    grad_drop = product(inner.T, upstream)
    grad_inner = product(upstream, hidden_drop.T)
    grad_gv = (grad_inner * lift_value * silu_grad(gate_value)).astype(jnp.bfloat16)
    grad_lv = (grad_inner * jax.nn.silu(gate_value)).astype(jnp.bfloat16)
    grad_gate = product(normed_two.T, grad_gv)
    grad_lift = product(normed_two.T, grad_lv)
    grad_two = product(grad_gv, hidden_gate.T) + product(grad_lv, hidden_lift.T)
    grad_second = lax.optimization_barrier(jnp.sum(grad_two * residual * scale_two, axis=0))
    grad_resid = upstream.astype(jnp.float32) + rms_back(residual, scale_two, second_gain, grad_two)
    resid_low = grad_resid.astype(jnp.bfloat16)
    grad_output = product(gated.T, resid_low)
    grad_gated = product(resid_low, project_out.T).reshape(length, H, DV)
    grad_gatein = (grad_gated * normed_head * silu_grad(gate_in)).astype(jnp.bfloat16)
    grad_normhead = grad_gated * jax.nn.silu(gate_in)
    grad_scale = lax.optimization_barrier(jnp.sum(grad_normhead * mixed * scale_head, axis=(0, 1)))
    grad_mixed_low = rms_back(mixed, scale_head, head_scale, grad_normhead).astype(jnp.bfloat16)
    grad_mixed = lax.optimization_barrier(grad_mixed_low).astype(jnp.float32)
    grad_query, grad_keys, grad_values, grad_log = attention_back(query, keys, values, log_decay, starts, grad_mixed)
    grad_act = jnp.concatenate([grad_query * root, grad_keys, grad_values], axis=-1)
    grad_filtered = grad_act * silu_grad(filtered)
    grad_projected, grad_taps = conv_back(padded, filter_taps, grad_filtered)
    grad_projected = grad_projected.astype(jnp.bfloat16).reshape(length, H * QKV)
    grad_logits = grad_log.reshape(length, H * DK) * jax.nn.sigmoid(-logits) / NORMALIZER
    grad_bias = lax.optimization_barrier(jnp.sum(grad_logits, axis=0))
    logits_low = grad_logits.astype(jnp.bfloat16)
    grad_expand = product(squeezed.T, logits_low)
    squeeze_low = jnp.einsum('lhc,rhc->hlr', logits_low.reshape(length, H, DK).astype(jnp.float32), expand.reshape(RANK, H, DK).astype(jnp.float32), precision=HIGH).astype(jnp.bfloat16)
    squeeze_wide = squeeze_low.astype(jnp.float32)
    grad_squeeze = jnp.einsum('ld,hlr->dr', normed_one.astype(jnp.float32), squeeze_wide, precision=HIGH)
    grad_project = product(normed_one.T, grad_projected).reshape(D, H, QKV)
    gatein_flat = grad_gatein.reshape(length, H * DV)
    grad_gating = product(normed_one.T, gatein_flat)
    grad_one = product(grad_projected, weight_in.T) + product(gatein_flat, gating.T)
    grad_one = grad_one + jnp.einsum('hlr,dr->ld', squeeze_wide, squeeze.astype(jnp.float32), precision=HIGH)
    grad_first = lax.optimization_barrier(jnp.sum(grad_one * residual_in * scale_one, axis=0))
    input_grad = grad_resid + rms_back(residual_in, scale_one, first_gain, grad_one)
    grads = (grad_first, grad_project, grad_taps, grad_squeeze, grad_expand, grad_bias, grad_gating, grad_scale, grad_output, grad_second, grad_gate, grad_lift, grad_drop)
    return (block_out, input_grad, grads)

def reference(block_in, upstream, first_gain, project_in, filter_taps, squeeze, expand, decay_bias, gating, head_scale, project_out, second_gain, hidden_gate, hidden_lift, hidden_drop):
    outputs = []
    in_grads = []
    totals = None
    for index in range(SEQS):
        block_out, input_grad, grads = one_sequence(block_in[index], upstream[index], first_gain, project_in, filter_taps, squeeze, expand, decay_bias, gating, head_scale, project_out, second_gain, hidden_gate, hidden_lift, hidden_drop)
        outputs.append(block_out)
        in_grads.append(input_grad)
        if totals is None:
            totals = grads
        else:
            totals = tuple((left + right for left, right in zip(totals, grads)))
    return (jnp.stack(outputs), jnp.stack(in_grads), totals[0], totals[1], totals[2], totals[3], totals[4], totals[5], totals[6], totals[7], totals[8], totals[9], totals[10], totals[11], totals[12])
```

```python
import functools

import jax
import jax.numpy as jnp
from jax import lax
from jax.experimental import pallas as pl
from jax.experimental.pallas import tpu as pltpu
from jax.sharding import PartitionSpec as P

GROUP = 64


EPS = 1e-05
NORMALIZER = 16.0
HIGH = lax.Precision.HIGHEST


MESH = pl.DeviceIdType.MESH
PIECES = 4


def greet(devices):
    barrier = pltpu.get_barrier_semaphore()
    for device in devices:
        pl.semaphore_signal(barrier, inc=1, device_id=device, device_id_type=MESH)
    pl.semaphore_wait(barrier, len(devices))


def ring_kernel(size, arrays, *refs):
    ins, outs = refs[:arrays], refs[arrays : 2 * arrays]
    slots = refs[2 * arrays : 3 * arrays]
    send_sem, recv_sem = refs[3 * arrays :]
    half = size // 2
    me = lax.axis_index("seq")
    mine_head = lax.axis_index("head")
    low, high = me % 2, me // 2
    place = high + low * (2 * half - 1 - 2 * high)

    def member(position):
        position = (position + 2 * size) % size
        side = position // half
        return 2 * (position + side * (2 * half - 1 - 2 * position)) + side

    partners = (
        (member(place + 1), mine_head),
        (member(place - 1), mine_head),
    )
    greet(partners)
    rows = ins[0].shape[0] // size
    part = rows // 2

    def block(array, direction, position):
        start = pl.multiple_of(member(position) * rows + direction * part, part)
        return ins[array].at[pl.ds(start, part)]

    def copy(array, direction, step, source):
        return pltpu.make_async_remote_copy(
            src_ref=source,
            dst_ref=slots[array].at[direction, step],
            send_sem=send_sem.at[array, direction, step],
            recv_sem=recv_sem.at[array, direction, step],
            device_id=partners[direction],
            device_id_type=MESH,
        )

    for array in range(arrays):
        for direction, sign in ((0, 1), (1, -1)):
            copy(array, direction, 0, block(array, direction, place - sign)).start()

    def lap(step, carry):
        for array in range(arrays):
            for direction, sign in ((0, 1), (1, -1)):
                slot = slots[array].at[direction, step - 1]
                copy(array, direction, step - 1, slot).wait_recv()
                local = block(array, direction, place - sign * (step + 1))
                slot[...] = slot[...] + local[...]
                copy(array, direction, step, slot).start()
        return carry

    lax.fori_loop(1, size - 1, lap, 0)
    for array in range(arrays):
        for direction in range(2):
            slot = slots[array].at[direction, size - 2]
            copy(array, direction, size - 2, slot).wait_recv()
            local = block(array, direction, place)
            outs[array][pl.ds(direction * part, part)] = slot[...] + local[...]

    def finish(step, carry):
        for array in range(arrays):
            for direction in range(2):
                copy(array, direction, step, slots[array].at[direction, step]).wait_send()
        return carry

    lax.fori_loop(0, size - 1, finish, 0)


def ring_scatter(*partials):
    size = lax.axis_size("seq")
    arrays = len(partials)
    rows = partials[0].shape[0] // size
    return pl.pallas_call(
        functools.partial(ring_kernel, size, arrays),
        out_shape=[jax.ShapeDtypeStruct((rows, x.shape[1]), jnp.float32) for x in partials],
        in_specs=[pl.BlockSpec(memory_space=pltpu.VMEM)] * arrays,
        out_specs=[pl.BlockSpec(memory_space=pltpu.VMEM)] * arrays,
        scratch_shapes=[
            pltpu.VMEM((2, size - 1, rows // 2, x.shape[1]), jnp.float32) for x in partials
        ]
        + [pltpu.SemaphoreType.DMA((arrays, 2, size - 1))] * 2,
        compiler_params=pltpu.CompilerParams(
            collective_id=0, has_side_effects=True, vmem_limit_bytes=56 * 1024 * 1024
        ),
    )(*partials)


def head_kernel(in_ref, out_ref, pair, summed, other, back, send_sem, recv_sem):
    me = lax.axis_index("head")
    mine_seq = lax.axis_index("seq")
    core, chip = me % 2, me // 2
    near = (mine_seq, chip * 2 + 1 - core)
    far = (mine_seq, (1 - chip) * 2 + core)
    greet((near, far))
    half = in_ref.shape[0] // 2
    piece = half // PIECES
    mine = pl.multiple_of(core * half, half)
    theirs = pl.multiple_of((1 - core) * half, half)

    def copy(stage, index, source, target, device):
        return pltpu.make_async_remote_copy(
            src_ref=source,
            dst_ref=target.at[pl.ds(index * piece, piece)],
            send_sem=send_sem.at[stage, index],
            recv_sem=recv_sem.at[stage, index],
            device_id=device,
            device_id_type=MESH,
        )

    first, second, third = [], [], []
    for index in range(PIECES):
        source = in_ref.at[pl.ds(theirs + index * piece, piece)]
        first.append(copy(0, index, source, pair, near))
        first[-1].start()
    for index in range(PIECES):
        rows = pl.ds(index * piece, piece)
        first[index].wait_recv()
        summed[rows] = in_ref[pl.ds(mine + index * piece, piece)] + pair[rows]
        second.append(copy(1, index, summed.at[rows], other, far))
        second[-1].start()
    for index in range(PIECES):
        rows = pl.ds(index * piece, piece)
        second[index].wait_recv()
        total = pl.ds(mine + index * piece, piece)
        out_ref[total] = summed[rows] + other[rows]
        third.append(copy(2, index, out_ref.at[total], back, near))
        third[-1].start()
    for index in range(PIECES):
        third[index].wait_recv()
        out_ref[pl.ds(theirs + index * piece, piece)] = back[pl.ds(index * piece, piece)]
    for item in first + second + third:
        item.wait_send()


def head_sum(value):
    rows, columns = value.shape
    landing = pltpu.VMEM((rows // 2, columns), jnp.float32)
    return pl.pallas_call(
        head_kernel,
        out_shape=jax.ShapeDtypeStruct(value.shape, jnp.float32),
        in_specs=[pl.BlockSpec(memory_space=pltpu.VMEM)],
        out_specs=pl.BlockSpec(memory_space=pltpu.VMEM),
        scratch_shapes=[landing] * 4 + [pltpu.SemaphoreType.DMA((3, PIECES))] * 2,
        compiler_params=pltpu.CompilerParams(
            collective_id=1, has_side_effects=True, vmem_limit_bytes=16 * 1024 * 1024
        ),
    )(value)


def shifted(x, axis, by):
    size = lax.axis_size(axis)
    pairs = [(i, i + by) for i in range(size) if 0 <= i + by < size]
    return lax.ppermute(x, axis, pairs)


def entering(value, axis, join, neutral, backward):
    count, mine = (lax.axis_size(axis), lax.axis_index(axis))
    pieces = jax.tree.map(lambda part: lax.all_gather(part, axis), value)
    if backward:
        pieces = jax.tree.map(lambda part: part[::-1], pieces)
        mine = count - 1 - mine
    total = jax.tree.map(
        lambda part, zero: jnp.full_like(part, 0) + jnp.asarray(zero, part.dtype), value, neutral
    )

    def lap(position, total):
        longer = join(total, jax.tree.map(lambda part: part[position], pieces))
        return jax.tree.map(lambda new, old: jnp.where(position < mine, new, old), longer, total)

    return lax.fori_loop(0, count - 1, lap, total)


def product(left, right):
    return jnp.dot(left, right, preferred_element_type=jnp.float32)


def against(left, right):
    return lax.dot_general(
        left, right, (((1,), (1,)), ((), ())), preferred_element_type=jnp.float32
    )


def across(left, right):
    return lax.dot_general(
        left, right, (((0,), (0,)), ((), ())), preferred_element_type=jnp.float32
    )


def rms_scale(values):
    return lax.rsqrt(jnp.mean(values * values, axis=-1, keepdims=True) + EPS)


def rms_back(values, scale, gain, incoming):
    weighted = gain * incoming
    cube = scale * scale * scale
    return scale * weighted - values * cube * jnp.mean(values * weighted, axis=-1, keepdims=True)


def silu_grad(values):
    logistic = jax.nn.sigmoid(values)
    return logistic * (1.0 + values * (1.0 - logistic))


def causal_mask(size):
    rows = lax.broadcasted_iota(jnp.int32, (size, size), 0)
    columns = lax.broadcasted_iota(jnp.int32, (size, size), 1)
    return (columns <= rows).astype(jnp.float32)


def chain(earlier, later):
    return (earlier[0] * later[0], later[0][..., None] * earlier[1] + later[1])


def grouped(array, seqs, count):
    return array.reshape((seqs, count, GROUP) + array.shape[2:])


def local_states(decays, updates, backward):

    def step(carry, item):
        decay, update = item
        return (jnp.exp(decay)[..., None] * carry + update, carry)

    init = jnp.zeros_like(updates[:, 0])
    total, states = lax.scan(
        step, init, (jnp.moveaxis(decays, 1, 0), jnp.moveaxis(updates, 1, 0)), reverse=backward
    )
    return (jnp.moveaxis(states, 0, 1), total)


def body(
    block_in,
    upstream,
    first_gain,
    project_in,
    filter_taps,
    squeeze,
    expand,
    decay_bias,
    gating,
    head_scale,
    project_out,
    second_gain,
    hidden_gate,
    hidden_lift,
    hidden_drop,
):
    seqs, tokens, width = block_in.shape
    total_rows = seqs * tokens
    key_dim = expand.shape[1]
    value_dim = gating.shape[1]
    mixed_dim = project_in.shape[2]
    lags = filter_taps.shape[0] - 1
    count = tokens // GROUP
    taps = filter_taps.reshape(lags + 1, mixed_dim)
    weight_in = project_in.reshape(width, mixed_dim)
    residual_in = block_in.reshape(total_rows, width).astype(jnp.float32)
    scale_one = rms_scale(residual_in)
    normed_one = (residual_in * scale_one * first_gain).astype(jnp.bfloat16)
    projected = product(normed_one, weight_in).reshape(seqs, tokens, mixed_dim)
    before = shifted(projected[:, tokens - lags :], "seq", 1)
    padded = jnp.concatenate([before, projected], axis=1)
    filtered = taps[0] * projected
    for lag in range(1, lags + 1):
        filtered = filtered + taps[lag] * padded[:, lags - lag : lags - lag + tokens]
    activated_low = jax.nn.silu(filtered).astype(jnp.bfloat16)
    activated = lax.optimization_barrier(activated_low).astype(jnp.float32)
    root = key_dim ** (-0.5)
    query = grouped(activated[..., :key_dim] * root, seqs, count)
    keys = grouped(activated[..., key_dim : 2 * key_dim], seqs, count)
    values = grouped(activated[..., 2 * key_dim :], seqs, count)
    squeezed = product(normed_one, squeeze).astype(jnp.bfloat16)
    logits = product(squeezed, expand) + decay_bias
    log_decay = grouped(
        (jax.nn.log_sigmoid(logits) / NORMALIZER).reshape(seqs, tokens, key_dim), seqs, count
    )
    gate_in = product(normed_one, gating)
    mask = causal_mask(GROUP)
    running = jnp.einsum("ij,snjc->snic", mask, log_decay, precision=HIGH)
    last = running[:, :, -1]
    query_in = query * jnp.exp(running)
    key_in = keys * jnp.exp(-running)
    key_end = keys * jnp.exp(last[:, :, None] - running)
    scores = jnp.einsum("snic,snjc->snij", query_in, key_in, precision=HIGH) * mask
    updates = jnp.einsum("snjc,snjd->sncd", key_end, values, precision=HIGH)
    starts_zero, state_total = local_states(last, updates, False)
    decay_sum = jnp.sum(last, axis=1)
    decay_total = jnp.exp(decay_sum)
    identity = (jnp.ones_like(decay_total), jnp.zeros_like(state_total))
    incoming = entering((decay_total, state_total), "seq", chain, identity, False)[1]
    before_group = jnp.cumsum(last, axis=1) - last
    starts = starts_zero + jnp.exp(before_group)[..., None] * incoming[:, None]
    mixed = jnp.einsum("snij,snjd->snid", scores, values, precision=HIGH)
    mixed = mixed + jnp.einsum("snic,sncd->snid", query_in, starts, precision=HIGH)
    mixed = mixed.reshape(total_rows, value_dim)
    scale_head = rms_scale(mixed)
    normed_head = mixed * scale_head * head_scale
    gated = (normed_head * jax.nn.silu(gate_in)).astype(jnp.bfloat16)
    branch = head_sum(product(gated, project_out))
    residual = residual_in + branch
    scale_two = rms_scale(residual)
    normed_two = (residual * scale_two * second_gain).astype(jnp.bfloat16)
    gate_value = product(normed_two, hidden_gate)
    lift_value = product(normed_two, hidden_lift)
    inner = (jax.nn.silu(gate_value) * lift_value).astype(jnp.bfloat16)
    feed = head_sum(product(inner, hidden_drop))
    block_out = (residual + feed).astype(jnp.bfloat16).reshape(seqs, tokens, width)
    seed = upstream.reshape(total_rows, width)
    grad_drop = across(seed, inner)
    grad_inner = against(seed, hidden_drop)
    grad_gv = (grad_inner * lift_value * silu_grad(gate_value)).astype(jnp.bfloat16)
    grad_lv = (grad_inner * jax.nn.silu(gate_value)).astype(jnp.bfloat16)
    feed_both = across(normed_two, jnp.concatenate([grad_gv, grad_lv], axis=1))
    grad_two = head_sum(against(grad_gv, hidden_gate) + against(grad_lv, hidden_lift))
    grad_second = jnp.sum(grad_two * residual * scale_two, axis=0)
    grad_resid = seed.astype(jnp.float32) + rms_back(residual, scale_two, second_gain, grad_two)
    resid_low = grad_resid.astype(jnp.bfloat16)
    grad_output = across(resid_low, gated)
    grad_gated = against(resid_low, project_out)
    grad_gatein = (grad_gated * normed_head * silu_grad(gate_in)).astype(jnp.bfloat16)
    grad_normhead = grad_gated * jax.nn.silu(gate_in)
    grad_scale = jnp.sum(grad_normhead * mixed * scale_head, axis=0)
    grad_mixed_low = rms_back(mixed, scale_head, head_scale, grad_normhead).astype(jnp.bfloat16)
    grad_mixed = lax.optimization_barrier(grad_mixed_low).astype(jnp.float32)
    outgrad = grouped(grad_mixed.reshape(seqs, tokens, value_dim), seqs, count)
    query_end = jnp.einsum("snic,snid->sncd", query_in, outgrad, precision=HIGH)
    following_zero, back_total = local_states(last, query_end, True)
    after = entering((decay_total, back_total), "seq", chain, identity, True)[1]
    after_group = decay_sum[:, None] - jnp.cumsum(last, axis=1)
    following = following_zero + jnp.exp(after_group)[..., None] * after[:, None]
    inner_group = jnp.einsum("snid,snjd->snij", outgrad, values, precision=HIGH) * mask
    grad_query = jnp.exp(running) * (
        jnp.einsum("snij,snjc->snic", inner_group, key_in, precision=HIGH)
        + jnp.einsum("snid,sncd->snic", outgrad, starts, precision=HIGH)
    )
    grad_keys = jnp.exp(-running) * jnp.einsum(
        "snij,snic->snjc", inner_group, query_in, precision=HIGH
    )
    grad_keys = grad_keys + jnp.exp(last[:, :, None] - running) * jnp.einsum(
        "snjd,sncd->snjc", values, following, precision=HIGH
    )
    grad_values = jnp.einsum("snij,snid->snjd", scores, outgrad, precision=HIGH)
    grad_values = grad_values + jnp.einsum("snjc,sncd->snjd", key_end, following, precision=HIGH)
    grad_running = (query * grad_query - keys * grad_keys).reshape(seqs, tokens, key_dim)
    state_end = decay_total[..., None] * incoming + state_total
    beyond = jnp.sum(state_end * after, axis=-1)
    upper = jnp.transpose(causal_mask(tokens))
    suffix = jnp.einsum("ij,sjc->sic", upper, grad_running, precision=HIGH)
    grad_log = suffix + beyond[:, None]
    grad_act = jnp.concatenate(
        [
            grad_query.reshape(seqs, tokens, key_dim) * root,
            grad_keys.reshape(seqs, tokens, key_dim),
            grad_values.reshape(seqs, tokens, value_dim),
        ],
        axis=-1,
    )
    grad_filtered = grad_act * silu_grad(filtered)
    later = shifted(grad_filtered[:, :lags], "seq", -1)
    padded_back = jnp.concatenate([grad_filtered, later], axis=1)
    grad_projected = taps[0] * grad_filtered
    tap_rows = [jnp.sum(grad_filtered * projected, axis=(0, 1))]
    for lag in range(1, lags + 1):
        grad_projected = grad_projected + taps[lag] * padded_back[:, lag : lag + tokens]
        tap_rows.append(
            jnp.sum(grad_filtered * padded[:, lags - lag : lags - lag + tokens], axis=(0, 1))
        )
    grad_taps = jnp.stack(tap_rows).reshape(lags + 1, 1, mixed_dim)
    grad_projected = grad_projected.reshape(total_rows, mixed_dim).astype(jnp.bfloat16)
    grad_logits = grad_log.reshape(total_rows, key_dim) * jax.nn.sigmoid(-logits) / NORMALIZER
    grad_bias = jnp.sum(grad_logits, axis=0)
    logits_low = grad_logits.astype(jnp.bfloat16)
    grad_expand = across(squeezed, logits_low)
    squeeze_low = against(logits_low, expand).astype(jnp.bfloat16)
    grad_squeeze = across(normed_one, squeeze_low)
    mixer_both = across(normed_one, jnp.concatenate([grad_projected, grad_gatein], axis=1))
    partial_value = (
        against(grad_projected, weight_in)
        + against(grad_gatein, gating)
        + against(squeeze_low, squeeze)
    )
    grad_one = head_sum(partial_value)
    grad_first = jnp.sum(grad_one * residual_in * scale_one, axis=0)
    input_grad = (grad_resid + rms_back(residual_in, scale_one, first_gain, grad_one)).reshape(
        seqs, tokens, width
    )
    feed_own, mixer_own, drop_own, output_own = ring_scatter(
        feed_both, mixer_both, grad_drop, grad_output
    )
    hidden = grad_gv.shape[1]
    summed = (
        mixer_own[:, None, :mixed_dim],
        mixer_own[:, mixed_dim:],
        jnp.transpose(output_own),
        feed_own[:, :hidden],
        feed_own[:, hidden:],
        jnp.transpose(drop_own),
    )
    small_head = lax.psum((grad_taps, grad_expand, grad_bias, grad_first, grad_second), "seq")
    shared = lax.psum((grad_scale, grad_squeeze), ("seq", "head"))
    return (
        block_out,
        input_grad,
        small_head[3],
        summed[0],
        small_head[0],
        shared[1],
        small_head[1],
        small_head[2],
        summed[1],
        shared[0],
        summed[2],
        small_head[4],
        summed[3],
        summed[4],
        summed[5],
    )


def solution(mesh):
    in_specs = (
        P(None, "seq", None),
        P(None, "seq", None),
        P(),
        P(None, "head", None),
        P(None, "head", None),
        P(),
        P(None, "head"),
        P("head"),
        P(None, "head"),
        P(),
        P("head", None),
        P(),
        P(None, "head"),
        P(None, "head"),
        P("head", None),
    )
    out_specs = (
        P(None, "seq", None),
        P(None, "seq", None),
        P(),
        P("seq", "head", None),
        P(None, "head", None),
        P(),
        P(None, "head"),
        P("head"),
        P("seq", "head"),
        P(),
        P("head", "seq"),
        P(),
        P("seq", "head"),
        P("seq", "head"),
        P("head", "seq"),
    )
    return jax.shard_map(body, mesh=mesh, in_specs=in_specs, out_specs=out_specs, check_vma=False)
```
